32 devices in a mesh: dp: 2 (over core), fsdp: 8 (over z, y), tensor: 2 (over x).
Axes of the slice: x: 2, y: 2, z: 4, core: 2. Of those that a mesh axis runs over, the one named last changes fastest.
Arguments:
- tokens: bfloat16 [4096, 4096], P(('dp', 'fsdp', 'tensor')), may hold values from -40 to 40
- norm_gain: float32 [4096], replicated, may hold values from 0.5 to 1.5
- tile_values: bfloat16 [464, 128, 128], P(('fsdp', 'tensor')), may hold values from -0.25 to 0.25
- tile_rows: int32 [2, 232], P('tensor'), may hold values from 0 to 31, as said below
- tile_cols: int32 [2, 232], P('tensor'), may hold values from 0 to 55
- tile_counts: int32 [2, 8], P('tensor'), may hold values from 0 to 29, as said below
- grad_out: bfloat16 [4096, 14336], P(('dp', 'fsdp'), 'tensor'), may hold values from -3 to 3
Outputs:
- mixed: bfloat16 [4096, 14336], P(('dp', 'fsdp'), 'tensor')
- grad_x: bfloat16 [4096, 4096], P(('dp', 'fsdp', 'tensor'))
- grad_gain: float32 [4096], replicated
- grad_tiles: float32 [464, 128, 128], P(('fsdp', 'tensor'))
The draws below stay inside these ranges and needn't reach their ends.
Inputs may be any that keep to these rules, and one draw needn't show every extreme that they name: `tile_counts`: for each tensor index the counts over the 8 fsdp shards sum to 224, and some shard holds exactly 29. `tile_rows`: within one tensor index the (row, column) pairs of held slots are all different.
All inputs are finite; a program needn't handle non-finite values.
Results may differ from the reference program's by a relative error of at most 0.013.
Values may be sent and summed in bfloat16 or wider, within the bound.
No kernel may reach another device: no remote copies, remote signals or barrier semaphores. Data moves between devices by JAX's collectives and lax.ppermute only.
A program may use at most 128 MiB of HBM per device.

```python
import jax
import jax.numpy as jnp
from jax import lax

TILE = 128
DW = 4096
FF = 14336
TOK_GRP = 256
TOKENS = 4096
FF_DEV = 7168
NNZ = 224
CAP = 29
N_DP = 2
N_FSDP = 8
N_TENSOR = 2


def tile_layout(key):
    row_tiles = DW // TILE
    col_tiles = FF // N_TENSOR // TILE
    slots_all = N_FSDP * CAP

    def one_shard(shard_key):
        key_one, key_two, key_three, key_four = jax.random.split(shard_key, 4)
        full_shard = jax.random.randint(key_one, (), 0, N_FSDP)
        shuffle = jax.random.permutation(key_two, slots_all)
        slot_shard = jnp.arange(slots_all) // CAP
        priority = jnp.where(slot_shard == full_shard, shuffle - slots_all, shuffle)
        slot_rank = jnp.argsort(jnp.argsort(priority))
        chosen = (slot_rank < NNZ).astype(jnp.int32)
        counts = jnp.sum(chosen.reshape(N_FSDP, CAP), axis=1).astype(jnp.int32)
        held = (jnp.arange(CAP)[None, :] < counts[:, None]).reshape(slots_all)
        positions = jax.random.permutation(key_three, row_tiles * col_tiles)[:NNZ]
        rank_held = jnp.clip(jnp.cumsum(held.astype(jnp.int32)) - 1, 0, NNZ - 1)
        unused_pos = jax.random.randint(key_four, (slots_all,), 0, row_tiles * col_tiles)
        position = jnp.where(held, positions[rank_held], unused_pos).astype(jnp.int32)
        return (position // col_tiles, position % col_tiles, counts)
    tensor_keys = jax.random.split(jax.random.fold_in(key, 7), N_TENSOR)
    return jax.vmap(one_shard)(tensor_keys)


def draw_tile_rows(key, part):
    return tile_layout(key)[0].astype(jnp.int32)


def draw_tile_cols(key, part):
    return tile_layout(key)[1].astype(jnp.int32)


def draw_tile_counts(key, part):
    return tile_layout(key)[2].astype(jnp.int32)


def draw_tokens(key, part):
    key_one, key_two, key_three = jax.random.split(jax.random.fold_in(key, 3), 3)
    row_scale = jnp.exp(jax.random.uniform(key_two, (TOKENS, 1), jnp.float32, -1.15, 1.15))
    col_scale = jnp.exp(jax.random.uniform(key_three, (1, DW), jnp.float32, -1.15, 1.15))
    base = jnp.clip(jax.random.normal(key_one, (TOKENS, DW), jnp.float32), -4.0, 4.0)
    return (base * row_scale * col_scale).astype(jnp.bfloat16)


def block_levels(own_key, extent, shards, least, high):
    loudness = 1.0
    for axis_at, blocks in shards:
        steps = jax.random.uniform(jax.random.fold_in(jax.random.fold_in(own_key, 6), axis_at), (blocks,), jnp.float32, least / len(shards), high / len(shards))
        loudness = loudness * jnp.repeat(jnp.exp(steps), extent[axis_at] // blocks).reshape((-1,) + (1,) * (len(extent) - 1 - axis_at))
    return loudness


def noise(stream_key, dims, spread, most, cuts=(), dtype=jnp.bfloat16):
    array = spread * jax.random.normal(stream_key, dims, jnp.float32)
    if cuts:
        array = array * block_levels(stream_key, dims, cuts, -0.22, 0.18)
    return jnp.clip(array, -most, most).astype(dtype)


def setup_inputs(seed: int = 0) -> dict:
    splits = jax.random.split(jax.random.key(seed), 8)
    return {
        "tokens": draw_tokens(jax.random.fold_in(splits[7], 71), 0),
        "norm_gain": jnp.clip(jax.random.uniform(splits[1], (DW,), jnp.float32, 0.5, 1.5), 0.5, 1.5),
        "tile_values": noise(splits[2], (N_FSDP * N_TENSOR * CAP, TILE, TILE), (DW // 8) ** -0.5, 0.25, ((0, 16),)),
        "tile_rows": draw_tile_rows(jax.random.fold_in(splits[7], 71), 0),
        "tile_cols": draw_tile_cols(jax.random.fold_in(splits[7], 71), 0),
        "tile_counts": draw_tile_counts(jax.random.fold_in(splits[7], 71), 0),
        "grad_out": noise(splits[6], (TOKENS, FF), 0.5, 3.0, ((0, 16), (1, 2))),
    }


def reference(tokens, norm_gain, tile_values, tile_rows, tile_cols, tile_counts, grad_out):
    local_float = tokens.astype(jnp.float32)
    inv_rms = lax.rsqrt(lax.optimization_barrier(jnp.mean(local_float * local_float, axis=1, keepdims=True)) + 1e-05)
    scaled = local_float * inv_rms
    normed = (scaled * norm_gain).astype(jnp.bfloat16)
    slots_all = N_FSDP * CAP
    row_tiles = DW // TILE
    col_tiles = FF_DEV // TILE
    groups = N_DP * N_FSDP
    values_by = tile_values.reshape(N_FSDP, N_TENSOR, CAP, TILE, TILE).transpose(1, 0, 2, 3, 4).reshape(N_TENSOR, slots_all, TILE, TILE)
    grad_by = grad_out.reshape(TOKENS, N_TENSOR, FF_DEV).transpose(1, 0, 2).reshape(N_TENSOR, groups, TOK_GRP, FF_DEV)
    x_groups = normed.astype(jnp.float32).reshape(groups, TOK_GRP, row_tiles, TILE)

    def per_shard(items):
        values, rows_list, cols_list, counts, grads = items
        held = (jnp.arange(CAP)[None, :] < counts[:, None]).reshape(slots_all)
        kept = jnp.where(held[:, None, None], values.astype(jnp.float32), jnp.float32(0.0))

        def per_group(pair):
            x_blocks, grad_rows = pair
            picked_x = jnp.take(x_blocks, rows_list, axis=1)
            product = jnp.einsum('tsk,skn->tsn', picked_x, kept)
            outputs = jnp.zeros((TOK_GRP, col_tiles, TILE), jnp.float32).at[:, cols_list].add(product)
            outputs = outputs.reshape(TOK_GRP, FF_DEV).astype(jnp.bfloat16)
            g_blocks = grad_rows.astype(jnp.float32).reshape(TOK_GRP, col_tiles, TILE)
            picked_g = jnp.take(g_blocks, cols_list, axis=1)
            backward = jnp.einsum('tsn,skn->tsk', picked_g, kept)
            partial_value = jnp.zeros((TOK_GRP, row_tiles, TILE), jnp.float32).at[:, rows_list].add(backward)
            partial_value = partial_value.reshape(TOK_GRP, DW).astype(jnp.bfloat16)
            terms = jnp.einsum('tsk,tsn->skn', picked_x, picked_g)
            return (outputs, partial_value, terms)
        outs_g, parts_g, terms_g = lax.map(per_group, (x_groups, grads))
        tile_grad = jnp.where(held[:, None, None], lax.optimization_barrier(jnp.sum(terms_g, axis=0)), jnp.float32(0.0))
        return (outs_g.reshape(TOKENS, FF_DEV), parts_g.reshape(TOKENS, DW), tile_grad)
    outs_all, partials, tile_grads = lax.map(per_shard, (values_by, tile_rows, tile_cols, tile_counts, grad_by))
    mixed = outs_all.transpose(1, 0, 2).reshape(TOKENS, FF)
    partials = lax.optimization_barrier(partials)
    input_grad = lax.optimization_barrier(jnp.sum(partials.astype(jnp.float32), axis=0))
    grad_gain = lax.optimization_barrier(jnp.sum(input_grad * scaled, axis=0))
    hidden_grad = input_grad * norm_gain
    grad_x = (inv_rms * (hidden_grad - scaled * lax.optimization_barrier(jnp.mean(hidden_grad * scaled, axis=1, keepdims=True)))).astype(jnp.bfloat16)
    grad_tiles = tile_grads.reshape(N_TENSOR, N_FSDP, CAP, TILE, TILE).transpose(1, 0, 2, 3, 4).reshape(N_FSDP * N_TENSOR * CAP, TILE, TILE)
    return (mixed, grad_x, grad_gain, grad_tiles)
```

```python
import functools

import jax
import jax.numpy as jnp
from jax import lax
from jax.experimental import pallas as pl
from jax.experimental.pallas import tpu as pltpu
from jax.sharding import PartitionSpec as P

F32 = jnp.float32
BF16 = jnp.bfloat16
VMEM = pl.BlockSpec(memory_space=pltpu.VMEM)
SMEM = pl.BlockSpec(memory_space=pltpu.SMEM)
HBM = pl.BlockSpec(memory_space=pl.ANY)
GRANT = 56 * 1024 * 1024


def lanes(index, size):
    return pl.ds(pl.multiple_of(index * size, size), size)


def divisor(count, most):
    return max(k for k in range(1, most + 1) if count % k == 0)


def part_rows(place, part, rows, parts):
    if parts == 1:
        return 0
    mine = place[3]
    start = mine if part == 0 else 1 - mine
    return pl.multiple_of(start * rows, rows)


def shard_of(place, z_shift, y_swap, z_size):
    z = lax.rem(place[0] + z_shift + z_size, z_size)
    y = place[1]
    return z * 2 + (1 - y if y_swap else y)


def norm_kernel(parts, *refs):
    place = refs[0]
    token_refs = refs[1 : 1 + parts]
    gain_ref, x_ref, xt_ref, inv_ref = refs[1 + parts :]
    for part, tok in enumerate(token_refs):
        rows, width = tok.shape
        start = part_rows(place, part, rows, parts)
        total = jnp.zeros((rows, 128), F32)
        for k in range(0, width, 128):
            v = tok[:, k : k + 128].astype(F32)
            total += v * v
        mean = jnp.sum(total, axis=1, keepdims=True) / width
        inv = lax.rsqrt(mean + 1e-05)
        inv_ref[pl.ds(start, rows), :] = jnp.broadcast_to(inv, (rows, 128))
        for k in range(0, width, 128):
            v = tok[:, k : k + 128].astype(F32) * inv * gain_ref[:, k : k + 128]
            x_ref[pl.ds(start, rows), k : k + 128] = v.astype(BF16)
            xt_ref[k : k + 128, pl.ds(start, rows)] = v.T.astype(BF16)


def grad_kernel(plan, z_size, cap, half, added, *refs):
    place, rows_ref, cols_ref, xt_ref, g_ref = refs[:5]
    add_ref = refs[5] if added else None
    outs = refs[6:] if added else refs[5:]
    tile = 128
    unroll = divisor(half, 5)
    for out, (pieces, y_swap, keep) in zip(outs, plan):
        h = place[2] if keep else 1 - place[2]
        for at, s in enumerate(pieces):
            base = shard_of(place, s, y_swap, z_size) * cap + h * (cap - half)

            def body(i, carry, out=out, at=at, s=s, base=base):
                for u in range(unroll):
                    j = i * unroll + u
                    r = rows_ref[0, base + j]
                    c = cols_ref[0, base + j]
                    v = jnp.dot(
                        xt_ref[lanes(r, tile), :], g_ref[:, lanes(c, tile)],
                        preferred_element_type=F32,
                    )
                    if added:
                        v += add_ref[s * half + j].astype(F32)
                    out[at * half + j] = v.astype(out.dtype)
                return carry

            lax.fori_loop(0, half // unroll, body, 0)


def load_tiles(local_ref, piece_refs, held_ref, sems, cap, half):
    copies = [pltpu.make_async_copy(local_ref, held_ref.at[pl.ds(0, cap)], sems.at[0])]
    for k, ref in enumerate(piece_refs):
        copies.append(
            pltpu.make_async_copy(ref, held_ref.at[pl.ds(cap + k * half, half)], sems.at[k + 1])
        )
    for copy in copies:
        copy.start()
    return copies


def each_tile(place, counts_ref, copies, keys, z_size, cap, half, step):
    copies[0].wait()
    own = shard_of(place, 0, False, z_size)
    count = counts_ref[0, own]
    unroll = divisor(cap, 4)

    def local(i, carry):
        for u in range(unroll):
            j = i * unroll + u
            step(j, own * cap + j, j < count)
        return carry

    lax.fori_loop(0, cap // unroll, local, 0)
    unroll = divisor(half, 5)
    for k, (s, y_swap, mine) in enumerate(keys):
        copies[k + 1].wait()
        shard = shard_of(place, -s, y_swap, z_size)
        h = place[2] if mine else 1 - place[2]
        first = h * (cap - half)
        count = counts_ref[0, shard]
        skip = h * (2 * half - cap)

        def body(i, carry, k=k, first=first, shard=shard, count=count, skip=skip):
            for u in range(unroll):
                j = i * unroll + u
                held = jnp.logical_and(j >= skip, first + j < count)
                step(cap + k * half + j, shard * cap + first + j, held)
            return carry

        lax.fori_loop(0, half // unroll, body, 0)


def back_kernel(keys, z_size, cap, half, parts, *refs):
    place, rows_ref, cols_ref, counts_ref, g_ref, inv_ref = refs[:6]
    tokens = refs[6 : 6 + parts]
    local_ref = refs[6 + parts]
    pieces = refs[7 + parts : 7 + parts + len(keys)]
    outs = refs[7 + parts + len(keys) :]
    sent, gain_ref, held_ref, acc_ref, sems = outs[:parts], *outs[parts:]
    tile = 128
    spare = acc_ref.shape[1] // tile - 1
    copies = load_tiles(local_ref, pieces, held_ref, sems, cap, half)
    acc_ref[...] = jnp.zeros_like(acc_ref)

    def step(at, slot, held):
        r = jnp.where(held, rows_ref[0, slot], spare)
        c = cols_ref[0, slot]
        acc_ref[:, lanes(r, tile)] += lax.dot_general(
            g_ref[:, lanes(c, tile)], held_ref[at], (((1,), (1,)), ((), ())),
            preferred_element_type=F32,
        )

    each_tile(place, counts_ref, copies, keys, z_size, cap, half, step)
    for k in range(0, spare * tile, tile):
        total = jnp.zeros((1, tile), F32)
        for part in range(parts):
            rows = tokens[part].shape[0]
            start = part_rows(place, part, rows, parts)
            v = acc_ref[pl.ds(start, rows), k : k + tile].astype(BF16)
            sent[part][:, k : k + tile] = v
            scaled = tokens[part][:, k : k + tile].astype(F32) * inv_ref[pl.ds(start, rows), :]
            total += jnp.sum(v.astype(F32) * scaled, axis=0, keepdims=True)
        gain_ref[:, k : k + tile] = total


def forward_kernel(keys, z_size, cap, half, *refs):
    place, rows_ref, cols_ref, counts_ref, x_ref, local_ref = refs[:6]
    pieces = refs[6 : 6 + len(keys)]
    out_ref, held_ref, acc_ref, sems = refs[6 + len(keys) :]
    tile = 128
    spare = acc_ref.shape[1] // tile - 1
    copies = load_tiles(local_ref, pieces, held_ref, sems, cap, half)
    acc_ref[...] = jnp.zeros_like(acc_ref)

    def step(at, slot, held):
        r = rows_ref[0, slot]
        c = jnp.where(held, cols_ref[0, slot], spare)
        acc_ref[:, lanes(c, tile)] += jnp.dot(
            x_ref[:, lanes(r, tile)], held_ref[at], preferred_element_type=F32
        )

    each_tile(place, counts_ref, copies, keys, z_size, cap, half, step)
    for k in range(0, spare * tile, tile):
        out_ref[:, k : k + tile] = acc_ref[:, k : k + tile].astype(BF16)


def input_kernel(count, *refs):
    place, tok, gain_ref, inv_ref = refs[:4]
    partials = refs[4 : 4 + count]
    out_ref, h_ref = refs[4 + count :]
    rows, width = tok.shape
    start = pl.multiple_of(place[3] * rows, rows)
    inv = inv_ref[pl.ds(start, rows), :]
    total = jnp.zeros((rows, 128), F32)
    for k in range(0, width, 128):
        cut = slice(k, k + 128)
        h = sum(p[:, cut].astype(F32) for p in partials) * gain_ref[:, cut]
        h_ref[:, cut] = h
        total += h * (tok[:, cut].astype(F32) * inv)
    mean = jnp.sum(total, axis=1, keepdims=True) / width
    for k in range(0, width, 128):
        cut = slice(k, k + 128)
        scaled = tok[:, cut].astype(F32) * inv
        out_ref[:, cut] = (inv * (h_ref[:, cut] - scaled * mean)).astype(BF16)


def join_kernel(cap, half, z_size, place, counts_ref, mine_ref, other_ref, out_ref):
    d = place[2]
    off = cap - half
    count = counts_ref[0, shard_of(place, 0, False, z_size)]
    for ref, h in ((mine_ref, d), (other_ref, 1 - d)):
        for j in range(half):
            slot = h * off + j
            out_ref[slot] = jnp.where(slot < count, ref[j], 0.0)


def call(kernel, outs, ins, specs, scratch=(), flops=0, moved=0, out_specs=None):
    return pl.pallas_call(
        kernel,
        out_shape=outs,
        in_specs=specs,
        out_specs=jax.tree.map(lambda _: VMEM, outs),
        scratch_shapes=list(scratch),
        cost_estimate=pl.CostEstimate(flops=flops, bytes_accessed=moved, transcendentals=0),
        compiler_params=pltpu.CompilerParams(vmem_limit_bytes=GRANT),
    )(*ins)


def swap(size):
    return [(i, i ^ 1) for i in range(size)]


def total_over(value, axis, size):
    if size <= 8:
        terms = [value] + [
            lax.ppermute(value, axis, [(i, i ^ k) for i in range(size)]) for k in range(1, size)
        ]
        while len(terms) > 1:
            terms = [terms[i] + terms[i + 1] for i in range(0, len(terms), 2)]
        return terms[0]
    bit = 1
    while bit < size:
        value = value + lax.ppermute(value, axis, [(i, i ^ bit) for i in range(size)])
        bit *= 2
    return value


def per_device(sizes, tokens, norm_gain, tile_values, tile_rows, tile_cols, tile_counts, grad_out):
    n_fsdp, n_tensor = sizes["fsdp"], sizes["tensor"]
    z_size = n_fsdp // 2
    cap, tile = tile_values.shape[:2]
    half = (cap + 1) // 2
    own_rows, width = tokens.shape
    group, hidden = grad_out.shape
    sds = jax.ShapeDtypeStruct
    f = lax.axis_index("fsdp")
    d = lax.axis_index("dp")
    t = lax.axis_index("tensor")
    spot = lax.iota(jnp.int32, 4)
    place = jnp.where(
        spot == 0, f // 2, jnp.where(spot == 1, f % 2, jnp.where(spot == 2, d, t))
    ).astype(jnp.int32)
    gain = norm_gain.reshape(1, width)

    def along_z(value, s):
        perm = [(z * 2 + y, (z + s) % z_size * 2 + y) for z in range(z_size) for y in range(2)]
        return lax.ppermute(value, "fsdp", perm)

    def along_y(value):
        return lax.ppermute(value, "fsdp", swap(n_fsdp))

    def along_dp(value):
        return lax.ppermute(value, "dp", swap(2))

    if n_tensor == 2:
        token_parts = [tokens, lax.ppermute(tokens, "tensor", swap(2))]
    else:
        token_parts = [lax.all_gather(tokens, "tensor", axis=0, tiled=True)]
    parts = len(token_parts)
    part_size = token_parts[0].shape[0]

    own_half = lax.dynamic_slice_in_dim(tile_values, d * (cap - half), half, axis=0)
    pieces = {(0, False): own_half}
    pieces[0, True] = along_y(own_half)
    for s in range(1, z_size):
        pieces[s, False] = along_z(own_half, s)
    for s in range(1, z_size):
        pieces[s, True] = along_y(pieces[s, False])
    keys, held = [], []
    for (s, y_swap), piece in pieces.items():
        if (s, y_swap) != (0, False):
            keys += [(s, y_swap, True), (s, y_swap, False)]
            held += [piece, along_dp(piece)]

    x, xt, inv = call(
        functools.partial(norm_kernel, parts),
        (sds((group, width), BF16), sds((width, group), BF16), sds((group, 128), F32)),
        (place, *token_parts, gain),
        [SMEM] + [VMEM] * (parts + 1),
        moved=3 * group * width * 2,
    )

    order = list(range(z_size))
    one = 2 * half * tile * tile * group

    def grads(plan, dtypes, add=None):
        outs = tuple(
            sds((len(p[0]) * half, tile, tile), dt) for p, dt in zip(plan, dtypes)
        )
        count = sum(len(p[0]) for p in plan)
        ins = (place, tile_rows, tile_cols, xt, grad_out) + (() if add is None else (add,))
        return call(
            functools.partial(grad_kernel, plan, z_size, cap, half, add is not None),
            outs, ins, [SMEM] * 3 + [VMEM] * (len(ins) - 3),
            flops=4 * one * count, moved=xt.size * 2 + grad_out.size * 2 + count * half * tile * tile * 2,
        )

    (away,) = grads([(order, True, False)], [BF16])
    away = along_dp(away)
    out = grads([(order, False, False)] + [([s], False, True) for s in order], [BF16] + [F32] * z_size)
    near, kept = along_dp(out[0]), out[1:]
    sends = grads([([s], True, True) for s in order], [BF16] * z_size, away)
    from_y = [None] * z_size
    for s in order[1:] + order[:1]:
        from_y[s] = along_y(sends[s])
    sums = [
        kept[s] + near[s * half : (s + 1) * half].astype(F32) + from_y[s].astype(F32) for s in order
    ]
    final = sums[0]
    for s in order[1:]:
        final = final + along_z(sums[s].astype(BF16), s).astype(F32)
    grad_tiles = call(
        functools.partial(join_kernel, cap, half, z_size),
        sds((cap, tile, tile), F32),
        (place, tile_counts, final, along_dp(final)),
        [SMEM, SMEM, VMEM, VMEM],
        moved=3 * cap * tile * tile * 4,
    )

    held_shape = pltpu.VMEM((cap + len(keys) * half, tile, tile), BF16)
    sems = pltpu.SemaphoreType.DMA((len(keys) + 1,))
    weight = tile_values.size * n_fsdp
    back = call(
        functools.partial(back_kernel, keys, z_size, cap, half, parts),
        tuple(sds((part_size, width), BF16) for _ in range(parts)) + (sds((1, width), F32),),
        (place, tile_rows, tile_cols, tile_counts, grad_out, inv, *token_parts, tile_values, *held),
        [SMEM] * 4 + [VMEM] * (2 + parts) + [HBM] * (1 + len(held)),
        scratch=(held_shape, pltpu.VMEM((group, width + tile), F32), sems),
        flops=8 * weight * group, moved=weight * 2 + grad_out.size * 2,
    )
    partials, gain_part = back[:parts], back[parts]
    if n_tensor == 2:
        partials = [partials[0], lax.ppermute(partials[1], "tensor", swap(2))]
    else:
        partials = [lax.psum_scatter(partials[0], "tensor", scatter_dimension=0, tiled=True)]
    gain_sum = total_over(gain_part, "tensor", n_tensor)
    gain_sum = total_over(gain_sum, "dp", sizes["dp"])
    gain_sum = total_over(gain_sum, "fsdp", n_fsdp)
    mixed = call(
        functools.partial(forward_kernel, keys, z_size, cap, half),
        sds((group, hidden), BF16),
        (place, tile_rows, tile_cols, tile_counts, x, tile_values, *held),
        [SMEM] * 4 + [VMEM] + [HBM] * (1 + len(held)),
        scratch=(held_shape, pltpu.VMEM((group, hidden + tile), F32), sems),
        flops=8 * weight * group, moved=weight * 2 + grad_out.size * 2,
    )
    grad_x = call(
        functools.partial(input_kernel, len(partials)),
        sds((own_rows, width), BF16),
        (place, tokens, gain, inv, *partials),
        [SMEM] + [VMEM] * (3 + len(partials)),
        scratch=(pltpu.VMEM((own_rows, width), F32),),
        moved=4 * own_rows * width * 2,
    )
    return (mixed, grad_x, gain_sum.reshape(width), grad_tiles)


def solution(mesh):
    placed = (
        P(("dp", "fsdp", "tensor"), None),
        P(),
        P(("fsdp", "tensor"), None, None),
        P("tensor", None),
        P("tensor", None),
        P("tensor", None),
        P(("dp", "fsdp"), "tensor"),
    )
    return jax.shard_map(
        functools.partial(per_device, dict(mesh.shape)),
        mesh=mesh,
        in_specs=placed,
        out_specs=(
            P(("dp", "fsdp"), "tensor"),
            P(("dp", "fsdp", "tensor"), None),
            P(),
            P(("fsdp", "tensor"), None, None),
        ),
        check_vma=False,
    )
```
